256 devices in a mesh: replica: 32 (over z, y_hi, core), fsdp: 8 (over y_lo, x).
Axes of the slice: x: 4, y: 4 (y_hi: 2, y_lo: 2; y = y_hi * 2 + y_lo), z: 8, core: 2. Of those that a mesh axis runs over, the one named last changes fastest.
Arguments:
- params: float32 [32, 128, 5120], P('replica', 'fsdp'), may hold values from -0.012 to 0.012
- tracker: float32 [32, 128, 5120], P('replica', 'fsdp'), may hold values from -2.1 to 2.1
- last_grad: float32 [32, 128, 5120], P('replica', 'fsdp'), may hold values from -2.1 to 2.1
- first_moment: float32 [32, 128, 5120], P('replica', 'fsdp'), may hold values from -1.8 to 1.8
- second_moment: float32 [32, 128, 5120], P('replica', 'fsdp'), may hold values from 0.02 to 0.5
- local_grads: bfloat16 [4, 32, 8, 128, 5120], P(None, 'replica', 'fsdp'), may hold values from -6 to 6
Outputs:
- param_change: float32 [32, 128, 5120], P('replica', 'fsdp')
- moment_one: float32 [32, 128, 5120], P('replica', 'fsdp')
- moment_two: float32 [32, 128, 5120], P('replica', 'fsdp')
The draws below stay inside these ranges and needn't reach their ends.
All inputs are finite; a program needn't handle non-finite values.
Results may differ from the reference program's by a relative error of at most 0.0003.
Values sent between devices are 32-bit elements; how exact they have to be, the bound alone decides.
A program may use at most 64 MiB of HBM per device.

```python
import math
import jax
import jax.numpy as jnp
from jax import lax

D = 5120
STEPS = 4
ROWS = 128
REPLICAS = 32
N_REPLICA = 32
N_FSDP = 8


def strengthened(entries, stream_key, source, target, shards_of, factor):
    def block_of(dim):
        return (jnp.arange(entries.shape[dim]) // (entries.shape[dim] // shards_of)).reshape((-1,) + (1,) * (entries.ndim - 1 - dim))

    first = jax.random.permutation(stream_key, shards_of)[block_of(target)]
    other_side = (block_of(target) + shards_of // 2) % shards_of
    return jnp.where((block_of(source) == first) | (block_of(source) == other_side), factor * entries, entries)


def levels(key, dims, shards, low, high):
    gain, own = 1.0, jax.random.fold_in(key, 6)
    for dim, shards_of in shards:
        draws = jnp.exp(jax.random.uniform(jax.random.fold_in(own, dim), (shards_of,), jnp.float32, low / len(shards), high / len(shards)))
        gain = gain * jnp.repeat(draws, dims[dim] // shards_of).reshape([-1 if axis == dim else 1 for axis in range(len(dims))])
    return gain


def normal_values(rng, extent, width, most, pieces=(), dtype=jnp.bfloat16):
    result = jax.random.normal(rng, extent, jnp.float32) * width
    if len(pieces) > 0:
        result = levels(rng, extent, pieces, -0.22, 0.18) * result
    return jnp.clip(result, min=-most, max=most).astype(dtype)


def noise_with(own_key, shape, spread, bound, split, heavy, dtype=jnp.bfloat16):
    drawn = spread * jax.random.normal(own_key, shape, jnp.float32)
    if split:
        drawn = drawn * levels(own_key, shape, split, -0.22, 0.18)
    return jnp.clip(strengthened(drawn, jax.random.fold_in(own_key, 3), *heavy), -bound, bound).astype(dtype)


def setup_inputs(seed: int = 0) -> dict:
    seeds = jax.random.split(jax.random.key(seed), 7)
    params = normal_values(seeds[0], (REPLICAS, ROWS, D), 0.002, 0.012, ((0, 32), (1, 8)), jnp.float32)
    tracker = normal_values(seeds[1], (REPLICAS, ROWS, D), 0.35, 2.1, ((0, 32), (1, 8)), jnp.float32)
    last_grad = normal_values(seeds[2], (REPLICAS, ROWS, D), 0.35, 2.1, ((0, 32), (1, 8)), jnp.float32)
    first_moment = normal_values(seeds[3], (REPLICAS, ROWS, D), 0.3, 1.8, ((0, 32), (1, 8)), jnp.float32)
    second_moment = jnp.clip(jnp.exp(math.log(0.5) - 3.218876 * jax.random.uniform(seeds[4], (REPLICAS, ROWS, D), jnp.float32) ** levels(seeds[4], (REPLICAS, ROWS, D), ((0, 32), (1, 8)), -0.2, 0.2)), 0.02, 0.5)
    local_grads = noise_with(seeds[5], (STEPS, REPLICAS, N_FSDP, ROWS, D), 1.0, 6.0, ((1, 32), (2, 8)), (2, 3, 8, 2.0))
    return {"params": params, "tracker": tracker, "last_grad": last_grad, "first_moment": first_moment, "second_moment": second_moment, "local_grads": local_grads}


LEARNING_RATE = 0.001
BETA_ONE = 0.9
BETA_TWO = 0.999
EPSILON = 1e-08

def reference(params, tracker, last_grad, first_moment, second_moment, local_grads):
    span_bits = N_REPLICA.bit_length() - 1
    weights = params
    tracking = tracker
    previous = last_grad
    moment_one = first_moment
    moment_two = second_moment
    for iteration in range(STEPS):
        distance = 2 ** (iteration % span_bits)
        mean_grad = lax.optimization_barrier(jnp.sum(local_grads[iteration].astype(jnp.float32), axis=1)) * (1.0 / N_FSDP)
        weights = 0.5 * (weights + jnp.roll(weights, distance, axis=0))
        tracking = 0.5 * (tracking + jnp.roll(tracking, distance, axis=0)) + mean_grad - previous
        previous = mean_grad
        moment_one = BETA_ONE * moment_one + (1.0 - BETA_ONE) * tracking
        moment_two = BETA_TWO * moment_two + (1.0 - BETA_TWO) * tracking * tracking
        weights = weights - LEARNING_RATE * moment_one / (jnp.sqrt(moment_two) + EPSILON)
    return ((weights - params) / LEARNING_RATE, moment_one, moment_two)
```

```python
import functools

import jax
import jax.numpy as jnp
from jax import lax
from jax.experimental import pallas as pl
from jax.experimental.pallas import tpu as pltpu
from jax.sharding import PartitionSpec as P

LEARNING_RATE = 0.001
BETA_ONE = 0.9
BETA_TWO = 0.999
EPSILON = 1e-08

MESH = pl.DeviceIdType.MESH
NX = 4
CHUNKS = 4
LEAD = 1


def item_order(steps, chunks):
    half = max(1, chunks // 2)
    groups = [range(0, half), range(half, chunks)]
    order = [(k, c) for group in groups for k in range(steps - 1) for c in group]
    return order + [(steps - 1, c) for c in range(chunks)]


def kernel(
    steps, replicas, order, width,
    params, tracker, last_grad, first_moment, second_moment, grads,
    out_change, out_one, out_two,
    gbuf, state, tw, twr, s1, sx, q, ra, rx, rd, re, rc,
    load_sem, state_sem, out_sem, send_sem, recv_sem, gsend_sem, grecv_sem,
):
    f32 = jnp.float32
    chunks = width // s1.shape[-1]
    cw = s1.shape[-1]
    r = lax.axis_index("replica")
    f = lax.axis_index("fsdp")
    y = f // NX
    x = lax.rem(f, NX)
    xm = lax.rem(x + NX - 1, NX)
    xp = lax.rem(x + 1, NX)
    x2 = lax.rem(x + 2, NX)
    oy = 1 - y

    def block(bx, by):
        return by * NX + bx

    to_xm = (r, block(xm, y))
    to_xp = (r, block(xp, y))
    to_y = (r, block(x, oy))
    shifts = [2 ** (k % (replicas.bit_length() - 1)) for k in range(steps)]

    barrier = pltpu.get_barrier_semaphore()
    feeders = [to_xm, to_xp, to_y] + [(lax.rem(r + replicas - s, replicas), f) for s in shifts]
    for dev in feeders:
        pl.semaphore_signal(barrier, inc=1, device_id=dev, device_id_type=MESH)

    def cols(c):
        return pl.ds(c * cw, cw)

    def state_loads(c):
        src = [tracker, params, last_grad, first_moment, second_moment]
        dst = [tw.at[0, c, 0], tw.at[0, c, 1], state.at[c, 0], state.at[c, 1], state.at[c, 2]]
        return [
            pltpu.make_async_copy(a.at[:, cols(c)], b, state_sem.at[c, n])
            for n, (a, b) in enumerate(zip(src, dst))
        ]

    def grad_load(i):
        k, c = order[i]
        return pltpu.make_async_copy(grads.at[k, :, :, cols(c)], gbuf.at[i], load_sem.at[i])

    grad_load(0).start()
    for c in range(chunks):
        for cp in state_loads(c)[:2]:
            cp.start()
    for i in range(1, len(order)):
        grad_load(i).start()
    for c in range(chunks):
        for cp in state_loads(c)[2:]:
            cp.start()

    sent = []

    def send(i, n, src, dst, dev):
        cp = pltpu.make_async_remote_copy(
            src_ref=src, dst_ref=dst, send_sem=send_sem.at[i, n], recv_sem=recv_sem.at[i, n],
            device_id=dev, device_id_type=MESH,
        )
        cp.start()
        sent.append(cp)

    def arrived(i, n, dst):
        pltpu.make_async_copy(dst, dst, recv_sem.at[i, n]).wait()

    def gossip(k, c):
        return pltpu.make_async_remote_copy(
            src_ref=tw.at[k, c], dst_ref=twr.at[k, c], send_sem=gsend_sem.at[k, c], recv_sem=grecv_sem.at[k, c],
            device_id=(lax.rem(r + shifts[k], replicas), f), device_id_type=MESH,
        )

    def raw(i, blk):
        return gbuf[i, blk].astype(f32)

    def fill(i):
        grad_load(i).wait()
        s1[i] = raw(i, block(x2, oy))
        sx[i, 0, 0:16] = raw(i, block(xm, oy))
        sx[i, 0, 16:24] = raw(i, block(xm, y))[8:16]
        sx[i, 1, 0:16] = raw(i, block(xp, oy))
        sx[i, 1, 16:24] = raw(i, block(xp, y))[0:8]

    def phase_one(i):
        send(i, 0, s1.at[i], ra.at[i], to_y)
        send(i, 1, sx.at[i, 0], rx.at[i, 0], to_xm)
        send(i, 2, sx.at[i, 1], rx.at[i, 1], to_xp)

    def phase_two(i):
        arrived(i, 0, ra.at[i])
        ra[i] = ra[i] + raw(i, block(x2, y))
        arrived(i, 1, rx.at[i, 0])
        arrived(i, 2, rx.at[i, 1])
        send(i, 3, ra.at[i, 0:8], rd.at[i, 0], to_xm)
        send(i, 4, ra.at[i, 8:16], rd.at[i, 1], to_xp)
        q[i] = raw(i, block(x, oy)) + rx[i, 0, 0:16] + rx[i, 1, 0:16]
        send(i, 5, q.at[i], re.at[i], to_y)

    def phase_three(i):
        arrived(i, 3, rd.at[i, 0])
        rd[i, 0] = rd[i, 0] + raw(i, block(xm, y))[0:8]
        send(i, 6, rd.at[i, 0], rc.at[i, 0], to_xm)
        arrived(i, 4, rd.at[i, 1])
        rd[i, 1] = rd[i, 1] + raw(i, block(xp, y))[8:16]
        send(i, 7, rd.at[i, 1], rc.at[i, 1], to_xp)

    def phase_four(i):
        k, c = order[i]
        arrived(i, 5, re.at[i])
        arrived(i, 6, rc.at[i, 0])
        arrived(i, 7, rc.at[i, 1])
        if k == 0:
            for cp in state_loads(c)[2:]:
                cp.wait()
        gossip(k, c).wait_recv()
        own = raw(i, block(x, y))
        for h in range(2):
            rows = slice(8 * h, 8 * h + 8)
            near, far = (rc[i, 0], rx[i, 1, 16:24]) if h == 0 else (rx[i, 0, 16:24], rc[i, 1])
            mean = (own[rows] + near + far + re[i, rows]) * (1.0 / 8.0)
            track = 0.5 * (tw[k, c, 0, rows] + twr[k, c, 0, rows]) + mean - state[c, 0, rows]
            one = BETA_ONE * state[c, 1, rows] + (1.0 - BETA_ONE) * track
            two = BETA_TWO * state[c, 2, rows] + (1.0 - BETA_TWO) * track * track
            weights = 0.5 * (tw[k, c, 1, rows] + twr[k, c, 1, rows])
            weights = weights - LEARNING_RATE * one / (jnp.sqrt(two) + EPSILON)
            if k + 1 < steps:
                state[c, 0, rows] = mean
                state[c, 1, rows] = one
                state[c, 2, rows] = two
                tw[k + 1, c, 0, rows] = track
                tw[k + 1, c, 1, rows] = weights
            else:
                state[c, 0, rows] = (weights - tw[0, c, 1, rows]) / LEARNING_RATE
                state[c, 1, rows] = one
                state[c, 2, rows] = two
        if k + 1 < steps:
            cp = gossip(k + 1, c)
            cp.start()
        else:
            for n, out in enumerate((out_change, out_one, out_two)):
                pltpu.make_async_copy(state.at[c, n], out.at[:, cols(c)], out_sem.at[c, n]).start()

    count = len(order)
    fill(0)
    pl.semaphore_wait(barrier, len(feeders))
    phase_one(0)
    for c in range(chunks):
        for cp in state_loads(c)[:2]:
            cp.wait()
        gossip(0, c).start()
    for i in range(1, LEAD):
        fill(i)
        phase_one(i)
    for t in range(LEAD, count + 2 + LEAD):
        if t < count:
            fill(t)
            phase_one(t)
        if 0 <= t - LEAD < count:
            phase_two(t - LEAD)
        if 0 <= t - LEAD - 1 < count:
            phase_three(t - LEAD - 1)
        if 0 <= t - LEAD - 2 < count:
            phase_four(t - LEAD - 2)

    for cp in sent:
        cp.wait_send()
    for k in range(steps):
        for c in range(chunks):
            gossip(k, c).wait_send()
    for c in range(chunks):
        for n, out in enumerate((out_change, out_one, out_two)):
            pltpu.make_async_copy(state.at[c, n], out.at[:, cols(c)], out_sem.at[c, n]).wait()


def per_device(params, tracker, last_grad, first_moment, second_moment, local_grads):
    rows, width = params.shape[1:]
    steps = local_grads.shape[0]
    shards = lax.axis_size("fsdp")
    replicas = lax.axis_size("replica")
    order = item_order(steps, CHUNKS)
    count = len(order)
    cw = width // CHUNKS
    f32 = jnp.float32
    block = jax.ShapeDtypeStruct((rows, width), f32)
    any_spec = pl.BlockSpec(memory_space=pl.ANY)
    change, one, two = pl.pallas_call(
        functools.partial(kernel, steps, replicas, order, width),
        out_shape=(block, block, block),
        in_specs=[any_spec] * 6,
        out_specs=(any_spec,) * 3,
        scratch_shapes=[
            pltpu.VMEM((count, shards, rows, cw), jnp.bfloat16),
            pltpu.VMEM((CHUNKS, 3, rows, cw), f32),
            pltpu.VMEM((steps, CHUNKS, 2, rows, cw), f32),
            pltpu.VMEM((steps, CHUNKS, 2, rows, cw), f32),
            pltpu.VMEM((count, 16, cw), f32),
            pltpu.VMEM((count, 2, 24, cw), f32),
            pltpu.VMEM((count, 16, cw), f32),
            pltpu.VMEM((count, 16, cw), f32),
            pltpu.VMEM((count, 2, 24, cw), f32),
            pltpu.VMEM((count, 2, 8, cw), f32),
            pltpu.VMEM((count, 16, cw), f32),
            pltpu.VMEM((count, 2, 8, cw), f32),
            pltpu.SemaphoreType.DMA((count,)),
            pltpu.SemaphoreType.DMA((CHUNKS, 5)),
            pltpu.SemaphoreType.DMA((CHUNKS, 3)),
            pltpu.SemaphoreType.DMA((count, 8)),
            pltpu.SemaphoreType.DMA((count, 8)),
            pltpu.SemaphoreType.DMA((steps, CHUNKS)),
            pltpu.SemaphoreType.DMA((steps, CHUNKS)),
        ],
        compiler_params=pltpu.CompilerParams(
            collective_id=0, has_side_effects=True, vmem_limit_bytes=60 << 20
        ),
        name="gossip_window",
    )(
        params[0], tracker[0], last_grad[0], first_moment[0], second_moment[0],
        local_grads.reshape(steps, shards, rows, width),
    )
    return change[None], one[None], two[None]


def solution(mesh):
    in_specs = (P("replica", "fsdp", None),) * 5 + (P(None, "replica", "fsdp", None, None),)
    out_specs = (P("replica", "fsdp", None),) * 3
    return jax.shard_map(
        per_device, mesh=mesh, in_specs=in_specs, out_specs=out_specs, check_vma=False
    )
```

```python
import functools

import jax
import jax.numpy as jnp
from jax import lax
from jax.experimental import pallas as pl
from jax.experimental.pallas import tpu as pltpu
from jax.sharding import PartitionSpec as P

LEARNING_RATE = 0.001
BETA_ONE = 0.9
BETA_TWO = 0.999
EPSILON = 1e-08

MESH = pl.DeviceIdType.MESH
RELAYED = (8,)
NX = 4
WIDTHS = [1152, 1152, 1024, 1024, 768]
ITEMS = [
    (0, 4), (0, 2), (1, 4), (2, 4), (1, 2), (2, 2), (0, 1), (0, 0), (1, 1), (0, 3), (2, 1), (1, 0), (1, 3),
    (2, 3), (2, 0), (3, 2), (3, 0), (3, 1), (3, 4), (3, 3),
]
X_FIRST = [4, 5, 11]
PROGRAM = [
    (0, 2), (1, 0), (1, 1), (1, 2), (1, 3), (0, 4), (0, 1), (2, 0), (0, 3), (2, 1), (1, 4), (3, 0), (2, 2),
    (3, 1), (2, 4), (1, 5), (1, 6), (4, 0), (3, 2), (4, 1), (2, 5), (3, 4), (2, 3), (0, 0), (2, 6), (1, 7),
    (4, 2), (3, 5), (3, 3), (3, 6), (4, 4), (1, 8), (1, 9), (4, 3), (2, 7), (4, 6), (1, 10), (4, 5), (2, 8),
    (3, 7), (5, 4), (2, 9), (1, 11), (4, 7), (3, 8), (2, 10), (3, 9), (2, 11), (1, 12), (5, 2), (4, 8), (3,
    10), (1, 13), (3, 11), (1, 14), (4, 9), (2, 12), (4, 10), (1, 15), (4, 11), (2, 14), (3, 12), (2, 13), (1,
    16), (5, 1), (3, 14), (1, 17), (3, 13), (4, 12), (1, 18), (2, 15), (4, 14), (1, 19), (4, 13), (2, 18), (2,
    16), (2, 17), (5, 0), (3, 15), (2, 19), (3, 16), (5, 3), (3, 17), (3, 18), (4, 15), (3, 19), (4, 16), (4,
    17), (4, 18), (4, 19),
]
FINISH_TILES = 2


def kernel(
    steps, replicas, shards, chunks,
    params, tracker, last_grad, first_moment, second_moment, grads,
    out_track, out_mix, out_one, out_two,
    gbuf, state, tw, twr, last, s1, sx, q, ra, rx, rd, re, rc,
    load_sem, state_sem, out_sem, send_sem, recv_sem, gsend_sem, grecv_sem, hop, hsend_sem, hrecv_sem,
):
    f32 = jnp.float32
    r = lax.axis_index("replica")
    f = lax.axis_index("fsdp")
    y = f // NX
    x = lax.rem(f, NX)
    xm = lax.rem(x + NX - 1, NX)
    xp = lax.rem(x + 1, NX)
    x2 = lax.rem(x + 2, NX)
    oy = 1 - y

    def block(bx, by):
        return by * NX + bx

    to_xm = (r, block(xm, y))
    to_xp = (r, block(xp, y))
    to_y = (r, block(x, oy))
    sides = ((xm, to_xm), (xp, to_xp))
    low, high = slice(0, 8), slice(8, 16)
    shifts = [2 ** (k % (replicas.bit_length() - 1)) for k in range(steps)]
    hops = [shifts[k] // 2 if shifts[k] in RELAYED else shifts[k] for k in range(steps)]

    barrier = pltpu.get_barrier_semaphore()
    feeders = [to_xm, to_xp, to_y]
    feeders += [(lax.rem(r + replicas - s, replicas), f) for s in sorted(set(hops))]
    for dev in feeders:
        pl.semaphore_signal(barrier, inc=1, device_id=dev, device_id_type=MESH)

    def cols(c):
        return pl.ds(chunks[c][0], chunks[c][1])

    def state_load(c, n):
        src = (tracker, params, last_grad, first_moment, second_moment)[n]
        dst = tw.at[0, n, :, cols(c)] if n < 2 else state.at[n - 2, :, cols(c)]
        return pltpu.make_async_copy(src.at[:, cols(c)], dst, state_sem.at[c, n])

    def grad_load(i):
        k, c = ITEMS[i]
        return pltpu.make_async_copy(grads.at[k, :, :, cols(c)], gbuf.at[k, :, :, cols(c)], load_sem.at[i])

    sent = []

    def send(i, n, src, dst, dev):
        cp = pltpu.make_async_remote_copy(
            src_ref=src, dst_ref=dst, send_sem=send_sem.at[i, n], recv_sem=recv_sem.at[i, n],
            device_id=dev, device_id_type=MESH,
        )
        cp.start()
        sent.append(cp)

    def arrived(i, n, dst):
        pltpu.make_async_copy(dst, dst, recv_sem.at[i, n]).wait()

    def gossip(k, c, final=True):
        direct = final and hops[k] == shifts[k]
        src = tw if direct or not final else hop
        dst = twr if final else hop
        sems = (gsend_sem, grecv_sem) if final else (hsend_sem, hrecv_sem)
        return pltpu.make_async_remote_copy(
            src_ref=(src.at[k] if src is tw else src.at[0]).at[:, :, cols(c)],
            dst_ref=(dst.at[k] if dst is twr else dst.at[0]).at[:, :, cols(c)],
            send_sem=sems[0].at[k, c], recv_sem=sems[1].at[k, c],
            device_id=(lax.rem(r + hops[k], replicas), f), device_id_type=MESH,
        )

    def start_gossip(k, c):
        gossip(k, c, hops[k] == shifts[k]).start()

    def relay(c):
        for k in range(steps):
            if hops[k] != shifts[k]:
                gossip(k, c, False).wait_recv()
                gossip(k, c).start()

    def raw(i, bx, by):
        k, c = ITEMS[i]
        return gbuf[k, block(bx, by), :, cols(c)].astype(f32)

    def fill(i):
        k, c = ITEMS[i]
        cc = cols(c)
        grad_load(i).wait()
        if i in X_FIRST:
            for n, (bx, _) in enumerate(sides):
                ours, theirs = (low, high) if n == 0 else (high, low)
                for b, by in enumerate((y, oy)):
                    sx[k, n, 8 * b : 8 * b + 8, cc] = raw(i, x2, by)[ours]
                    sx[k, n, 16 + 8 * b : 24 + 8 * b, cc] = raw(i, bx, by)[theirs]
        else:
            s1[k, :, cc] = raw(i, x2, oy)
            for n, (bx, _) in enumerate(sides):
                sx[k, n, 0:16, cc] = raw(i, bx, oy)
                sx[k, n, 16:24, cc] = raw(i, bx, y)[high if n == 0 else low]

    def phase_one(i):
        k, c = ITEMS[i]
        cc = cols(c)
        if i in X_FIRST:
            for n, (_, dev) in enumerate(sides):
                send(i, 3 + n, sx.at[k, n, 0:16, cc], rx.at[k, n, 0:16, cc], dev)
            for n, (_, dev) in enumerate(sides):
                send(i, 1 + n, sx.at[k, n, 16:32, cc], rx.at[k, n, 16:32, cc], dev)
        else:
            send(i, 0, s1.at[k, :, cc], ra.at[k, :, cc], to_y)
            for n, (_, dev) in enumerate(sides):
                send(i, 1 + n, sx.at[k, n, 0:24, cc], rx.at[k, n, 0:24, cc], dev)

    def phase_two(i):
        k, c = ITEMS[i]
        cc = cols(c)
        if i in X_FIRST:
            for n, (bx, dev) in enumerate(sides):
                arrived(i, 3 + n, rx.at[k, n, 0:16, cc])
                for b, by in enumerate((y, oy)):
                    rows = slice(8 * b, 8 * b + 8)
                    rx[k, n, rows, cc] = rx[k, n, rows, cc] + raw(i, bx, by)[low if n == 0 else high]
                send(i, 6 + n, rx.at[k, n, 0:16, cc], rc.at[k, n, :, cc], dev)
        else:
            arrived(i, 0, ra.at[k, :, cc])
            ra[k, :, cc] = ra[k, :, cc] + raw(i, x2, y)
            for n, (_, dev) in enumerate(sides):
                send(i, 3 + n, ra.at[k, 8 * n : 8 * n + 8, cc], rd.at[k, n, :, cc], dev)
            for n in range(2):
                arrived(i, 1 + n, rx.at[k, n, 0:24, cc])
            q[k, :, cc] = raw(i, x, oy) + rx[k, 0, 0:16, cc] + rx[k, 1, 0:16, cc]
            send(i, 5, q.at[k, :, cc], re.at[k, :, cc], to_y)

    def phase_three(i):
        k, c = ITEMS[i]
        cc = cols(c)
        if i in X_FIRST:
            for n in range(2):
                arrived(i, 1 + n, rx.at[k, n, 16:32, cc])
                arrived(i, 6 + n, rc.at[k, n, :, cc])
            mine = raw(i, x, oy)
            q[k, 0:8, cc] = mine[low] + rc[k, 0, 8:16, cc] + rx[k, 1, 24:32, cc]
            q[k, 8:16, cc] = mine[high] + rx[k, 0, 24:32, cc] + rc[k, 1, 8:16, cc]
            send(i, 5, q.at[k, :, cc], re.at[k, :, cc], to_y)
        else:
            for n, (bx, dev) in enumerate(sides):
                arrived(i, 3 + n, rd.at[k, n, :, cc])
                rd[k, n, :, cc] = rd[k, n, :, cc] + raw(i, bx, y)[low if n == 0 else high]
                send(i, 6 + n, rd.at[k, n, :, cc], rc.at[k, n, 0:8, cc], dev)

    def phase_four(i):
        k, c = ITEMS[i]
        cc = cols(c)
        if i not in X_FIRST:
            for n in range(2):
                arrived(i, 6 + n, rc.at[k, n, 0:8, cc])
        if k == 0:
            for n in range(2, 5):
                state_load(c, n).wait()
        gossip(k, c).wait_recv()
        arrived(i, 5, re.at[k, :, cc])
        mine = raw(i, x, y)
        for h, rows in enumerate((low, high)):
            near = rx[k, 1 - h, 16:24, cc]
            mean = (mine[rows] + rc[k, h, 0:8, cc] + near + re[k, rows, cc]) * (1.0 / shards)
            track = 0.5 * (tw[k, 0, rows, cc] + twr[k, 0, rows, cc]) + mean - state[0, rows, cc]
            mix = 0.5 * (tw[k, 1, rows, cc] + twr[k, 1, rows, cc])
            if k + 1 < steps:
                one = BETA_ONE * state[1, rows, cc] + (1.0 - BETA_ONE) * track
                two = BETA_TWO * state[2, rows, cc] + (1.0 - BETA_TWO) * track * track
                tw[k + 1, 0, rows, cc] = track
                tw[k + 1, 1, rows, cc] = mix - LEARNING_RATE * one / (jnp.sqrt(two) + EPSILON)
                state[0, rows, cc] = mean
                state[1, rows, cc] = one
                state[2, rows, cc] = two
            else:
                last[0, rows, cc] = track
                last[1, rows, cc] = mix
        if k + 1 < steps:
            start_gossip(k + 1, c)
        if k + 2 == steps:
            result(c, 2).start()
            result(c, 3).start()
        if k + 1 == steps:
            result(c, 0).start()
            result(c, 1).start()

    def result(c, n):
        src = last.at[n, :, cols(c)] if n < 2 else state.at[n - 1, :, cols(c)]
        dst = (out_track, out_mix, out_one, out_two)[n].at[:, cols(c)]
        return pltpu.make_async_copy(src, dst, out_sem.at[c, n])

    every = range(len(chunks))
    grad_load(0).start()
    for c in every:
        state_load(c, 0).start()
        state_load(c, 1).start()
    for i in range(1, len(ITEMS)):
        grad_load(i).start()
    for c in every:
        for n in range(2, 5):
            state_load(c, n).start()

    phases = (None, phase_one, phase_two, phase_three, phase_four)
    fill(0)
    pl.semaphore_wait(barrier, len(feeders))
    for phase, i in PROGRAM:
        if phase == 0:
            state_load(i, 0).wait()
            state_load(i, 1).wait()
            start_gossip(0, i)
        elif phase == 5:
            relay(i)
        else:
            phases[phase](i)
            if phase == 1 and i + 1 < len(ITEMS):
                fill(i + 1)

    for c in every:
        for n in range(4):
            result(c, n).wait()
    for cp in sent:
        cp.wait_send()
    for k in range(steps):
        for c in every:
            gossip(k, c).wait_send()
            if hops[k] != shifts[k]:
                gossip(k, c, False).wait_send()


def finish(track, mix, first, second, params, change, one, two):
    one[...] = BETA_ONE * first[...] + (1.0 - BETA_ONE) * track[...]
    two[...] = BETA_TWO * second[...] + (1.0 - BETA_TWO) * track[...] * track[...]
    weights = mix[...] - LEARNING_RATE * one[...] / (jnp.sqrt(two[...]) + EPSILON)
    change[...] = (weights - params[...]) / LEARNING_RATE


def per_device(params, tracker, last_grad, first_moment, second_moment, local_grads):
    rows, width = params.shape[1:]
    steps = local_grads.shape[0]
    shards = lax.axis_size("fsdp")
    replicas = lax.axis_size("replica")
    chunks = [(sum(WIDTHS[:c]), w) for c, w in enumerate(WIDTHS)]
    assert sum(WIDTHS) == width and len(ITEMS) == steps * len(WIDTHS)
    count = len(ITEMS)
    f32 = jnp.float32
    any_spec = pl.BlockSpec(memory_space=pl.ANY)
    track, mix, one, two = pl.pallas_call(
        functools.partial(kernel, steps, replicas, shards, chunks),
        out_shape=(jax.ShapeDtypeStruct((rows, width), f32),) * 4,
        in_specs=[any_spec] * 6,
        out_specs=(any_spec,) * 4,
        scratch_shapes=[
            pltpu.VMEM((steps, shards, rows, width), jnp.bfloat16),
            pltpu.VMEM((3, rows, width), f32),
            pltpu.VMEM((steps, 2, rows, width), f32),
            pltpu.VMEM((steps, 2, rows, width), f32),
            pltpu.VMEM((2, rows, width), f32),
            pltpu.VMEM((steps, 16, width), f32),
            pltpu.VMEM((steps, 2, 32, width), f32),
            pltpu.VMEM((steps, 16, width), f32),
            pltpu.VMEM((steps, 16, width), f32),
            pltpu.VMEM((steps, 2, 32, width), f32),
            pltpu.VMEM((steps, 2, 8, width), f32),
            pltpu.VMEM((steps, 16, width), f32),
            pltpu.VMEM((steps, 2, 16, width), f32),
            pltpu.SemaphoreType.DMA((count,)),
            pltpu.SemaphoreType.DMA((len(chunks), 5)),
            pltpu.SemaphoreType.DMA((len(chunks), 4)),
            pltpu.SemaphoreType.DMA((count, 8)),
            pltpu.SemaphoreType.DMA((count, 8)),
            pltpu.SemaphoreType.DMA((steps, len(chunks))),
            pltpu.SemaphoreType.DMA((steps, len(chunks))),
            pltpu.VMEM((1, 2, rows, width), f32),
            pltpu.SemaphoreType.DMA((steps, len(chunks))),
            pltpu.SemaphoreType.DMA((steps, len(chunks))),
        ],
        compiler_params=pltpu.CompilerParams(
            collective_id=0, has_side_effects=True, vmem_limit_bytes=60 << 20
        ),
        name="gossip_window",
    )(
        params[0], tracker[0], last_grad[0], first_moment[0], second_moment[0],
        local_grads.reshape(steps, shards, rows, width),
    )
    tile = pl.BlockSpec((rows, width // FINISH_TILES), lambda c: (0, c))
    block = jax.ShapeDtypeStruct((rows, width), f32)
    change, one, two = pl.pallas_call(
        finish,
        grid=(FINISH_TILES,),
        out_shape=(block,) * 3,
        in_specs=[tile] * 5,
        out_specs=(tile,) * 3,
        name="finish",
    )(track, mix, one, two, params[0])
    return change[None], one[None], two[None]


def solution(mesh):
    in_specs = (P("replica", "fsdp", None),) * 5 + (P(None, "replica", "fsdp", None, None),)
    out_specs = (P("replica", "fsdp", None),) * 3
    return jax.shard_map(
        per_device, mesh=mesh, in_specs=in_specs, out_specs=out_specs, check_vma=False
    )
```

```python
import functools

import jax
import jax.numpy as jnp
from jax import lax
from jax.experimental import pallas as pl
from jax.experimental.pallas import tpu as pltpu
from jax.sharding import PartitionSpec as P

LEARNING_RATE = 0.001
BETA_ONE = 0.9
BETA_TWO = 0.999
EPSILON = 1e-08

MESH = pl.DeviceIdType.MESH
RELAYED = (8,)
NX = 4
WIDTHS = [1152, 1152, 1024, 1024, 768]
ITEMS = [
    (0, 4), (1, 4), (0, 3), (1, 3), (2, 4), (0, 0), (2, 3), (0, 1), (1, 0), (0, 2), (2, 0), (1, 1), (1, 2),
    (2, 1), (2, 2), (3, 0), (3, 4), (3, 1), (3, 3), (3, 2),
]
X_FIRST = [5, 8, 4]
PROGRAM = [
    (1, 0), (1, 1), (1, 2), (0, 4), (0, 3), (2, 0), (1, 3), (2, 2), (2, 1), (3, 0), (1, 4), (0, 2), (3, 2),
    (1, 5), (2, 3), (4, 0), (4, 2), (2, 4), (3, 1), (2, 5), (1, 6), (0, 0), (3, 3), (1, 7), (4, 1), (3, 4),
    (3, 5), (0, 1), (2, 6), (1, 8), (4, 3), (4, 4), (3, 6), (2, 7), (1, 9), (2, 8), (4, 5), (4, 6), (3, 7),
    (5, 4), (1, 10), (3, 8), (2, 9), (1, 11), (4, 7), (2, 10), (1, 12), (4, 8), (3, 9), (2, 11), (3, 10), (5,
    3), (1, 13), (4, 9), (3, 11), (1, 14), (4, 10), (2, 12), (1, 15), (4, 11), (2, 13), (3, 12), (1, 16), (5,
    0), (2, 14), (3, 13), (1, 17), (4, 12), (3, 14), (1, 18), (4, 13), (1, 19), (2, 15), (2, 16), (4, 14), (2,
    18), (2, 17), (5, 1), (2, 19), (3, 15), (3, 16), (5, 2), (3, 18), (3, 17), (3, 19), (4, 15), (4, 16), (4,
    18), (4, 17), (4, 19),
]
FINISH_TILES = 2


def kernel(
    steps, replicas, shards, chunks,
    params, tracker, last_grad, first_moment, second_moment, grads,
    out_track, out_mix, out_one, out_two,
    gbuf, state, tw, twr, last, s1, sx, q, ra, rx, rd, re, rc,
    load_sem, state_sem, out_sem, send_sem, recv_sem, gsend_sem, grecv_sem, hop, hsend_sem, hrecv_sem,
):
    f32 = jnp.float32
    r = lax.axis_index("replica")
    f = lax.axis_index("fsdp")
    y = f // NX
    x = lax.rem(f, NX)
    xm = lax.rem(x + NX - 1, NX)
    xp = lax.rem(x + 1, NX)
    x2 = lax.rem(x + 2, NX)
    oy = 1 - y

    def block(bx, by):
        return by * NX + bx

    to_xm = (r, block(xm, y))
    to_xp = (r, block(xp, y))
    to_y = (r, block(x, oy))
    sides = ((xm, to_xm), (xp, to_xp))
    low, high = slice(0, 8), slice(8, 16)
    shifts = [2 ** (k % (replicas.bit_length() - 1)) for k in range(steps)]
    hops = [shifts[k] // 2 if shifts[k] in RELAYED else shifts[k] for k in range(steps)]

    barrier = pltpu.get_barrier_semaphore()
    feeders = [to_xm, to_xp, to_y]
    feeders += [(lax.rem(r + replicas - s, replicas), f) for s in sorted(set(hops))]
    for dev in feeders:
        pl.semaphore_signal(barrier, inc=1, device_id=dev, device_id_type=MESH)

    def cols(c):
        return pl.ds(chunks[c][0], chunks[c][1])

    def state_load(c, n):
        src = (tracker, params, last_grad, first_moment, second_moment)[n]
        dst = tw.at[0, n, :, cols(c)] if n < 2 else state.at[n - 2, :, cols(c)]
        return pltpu.make_async_copy(src.at[:, cols(c)], dst, state_sem.at[c, n])

    def grad_load(i):
        k, c = ITEMS[i]
        return pltpu.make_async_copy(grads.at[k, :, :, cols(c)], gbuf.at[k, :, :, cols(c)], load_sem.at[i])

    sent = []

    def send(i, n, src, dst, dev):
        cp = pltpu.make_async_remote_copy(
            src_ref=src, dst_ref=dst, send_sem=send_sem.at[i, n], recv_sem=recv_sem.at[i, n],
            device_id=dev, device_id_type=MESH,
        )
        cp.start()
        sent.append(cp)

    def arrived(i, n, dst):
        pltpu.make_async_copy(dst, dst, recv_sem.at[i, n]).wait()

    def gossip(k, c, final=True):
        direct = final and hops[k] == shifts[k]
        src = tw if direct or not final else hop
        dst = twr if final else hop
        sems = (gsend_sem, grecv_sem) if final else (hsend_sem, hrecv_sem)
        return pltpu.make_async_remote_copy(
            src_ref=(src.at[k] if src is tw else src.at[0]).at[:, :, cols(c)],
            dst_ref=(dst.at[k] if dst is twr else dst.at[0]).at[:, :, cols(c)],
            send_sem=sems[0].at[k, c], recv_sem=sems[1].at[k, c],
            device_id=(lax.rem(r + hops[k], replicas), f), device_id_type=MESH,
        )

    def start_gossip(k, c):
        gossip(k, c, hops[k] == shifts[k]).start()

    def relay(c):
        for k in range(steps):
            if hops[k] != shifts[k]:
                gossip(k, c, False).wait_recv()
                gossip(k, c).start()

    def raw(i, bx, by):
        k, c = ITEMS[i]
        return gbuf[k, block(bx, by), :, cols(c)].astype(f32)

    def fill(i):
        k, c = ITEMS[i]
        cc = cols(c)
        grad_load(i).wait()
        if i in X_FIRST:
            for n, (bx, _) in enumerate(sides):
                ours, theirs = (low, high) if n == 0 else (high, low)
                for b, by in enumerate((y, oy)):
                    sx[k, n, 8 * b : 8 * b + 8, cc] = raw(i, x2, by)[ours]
                    sx[k, n, 16 + 8 * b : 24 + 8 * b, cc] = raw(i, bx, by)[theirs]
        else:
            s1[k, :, cc] = raw(i, x2, oy)
            for n, (bx, _) in enumerate(sides):
                sx[k, n, 0:16, cc] = raw(i, bx, oy)
                sx[k, n, 16:24, cc] = raw(i, bx, y)[high if n == 0 else low]

    def phase_one(i):
        k, c = ITEMS[i]
        cc = cols(c)
        if i in X_FIRST:
            for n, (_, dev) in enumerate(sides):
                send(i, 3 + n, sx.at[k, n, 0:16, cc], rx.at[k, n, 0:16, cc], dev)
            for n, (_, dev) in enumerate(sides):
                send(i, 1 + n, sx.at[k, n, 16:32, cc], rx.at[k, n, 16:32, cc], dev)
        else:
            send(i, 0, s1.at[k, :, cc], ra.at[k, :, cc], to_y)
            for n, (_, dev) in enumerate(sides):
                send(i, 1 + n, sx.at[k, n, 0:24, cc], rx.at[k, n, 0:24, cc], dev)

    def phase_two(i):
        k, c = ITEMS[i]
        cc = cols(c)
        if i in X_FIRST:
            for n, (bx, dev) in enumerate(sides):
                arrived(i, 3 + n, rx.at[k, n, 0:16, cc])
                for b, by in enumerate((y, oy)):
                    rows = slice(8 * b, 8 * b + 8)
                    rx[k, n, rows, cc] = rx[k, n, rows, cc] + raw(i, bx, by)[low if n == 0 else high]
                send(i, 6 + n, rx.at[k, n, 0:16, cc], rc.at[k, n, :, cc], dev)
        else:
            arrived(i, 0, ra.at[k, :, cc])
            ra[k, :, cc] = ra[k, :, cc] + raw(i, x2, y)
            for n, (_, dev) in enumerate(sides):
                send(i, 3 + n, ra.at[k, 8 * n : 8 * n + 8, cc], rd.at[k, n, :, cc], dev)
            for n in range(2):
                arrived(i, 1 + n, rx.at[k, n, 0:24, cc])
            q[k, :, cc] = raw(i, x, oy) + rx[k, 0, 0:16, cc] + rx[k, 1, 0:16, cc]
            send(i, 5, q.at[k, :, cc], re.at[k, :, cc], to_y)

    def phase_three(i):
        k, c = ITEMS[i]
        cc = cols(c)
        if i in X_FIRST:
            for n in range(2):
                arrived(i, 1 + n, rx.at[k, n, 16:32, cc])
                arrived(i, 6 + n, rc.at[k, n, :, cc])
            mine = raw(i, x, oy)
            q[k, 0:8, cc] = mine[low] + rc[k, 0, 8:16, cc] + rx[k, 1, 24:32, cc]
            q[k, 8:16, cc] = mine[high] + rx[k, 0, 24:32, cc] + rc[k, 1, 8:16, cc]
            send(i, 5, q.at[k, :, cc], re.at[k, :, cc], to_y)
        else:
            for n, (bx, dev) in enumerate(sides):
                arrived(i, 3 + n, rd.at[k, n, :, cc])
                rd[k, n, :, cc] = rd[k, n, :, cc] + raw(i, bx, y)[low if n == 0 else high]
                send(i, 6 + n, rd.at[k, n, :, cc], rc.at[k, n, 0:8, cc], dev)

    def phase_four(i):
        k, c = ITEMS[i]
        cc = cols(c)
        if i not in X_FIRST:
            for n in range(2):
                arrived(i, 6 + n, rc.at[k, n, 0:8, cc])
        if k == 0:
            for n in range(2, 5):
                state_load(c, n).wait()
        gossip(k, c).wait_recv()
        arrived(i, 5, re.at[k, :, cc])
        mine = raw(i, x, y)
        for h, rows in enumerate((low, high)):
            near = rx[k, 1 - h, 16:24, cc]
            mean = (mine[rows] + rc[k, h, 0:8, cc] + near + re[k, rows, cc]) * (1.0 / shards)
            track = 0.5 * (tw[k, 0, rows, cc] + twr[k, 0, rows, cc]) + mean - state[0, rows, cc]
            mix = 0.5 * (tw[k, 1, rows, cc] + twr[k, 1, rows, cc])
            if k + 1 < steps:
                one = BETA_ONE * state[1, rows, cc] + (1.0 - BETA_ONE) * track
                two = BETA_TWO * state[2, rows, cc] + (1.0 - BETA_TWO) * track * track
                tw[k + 1, 0, rows, cc] = track
                tw[k + 1, 1, rows, cc] = mix - LEARNING_RATE * one / (jnp.sqrt(two) + EPSILON)
                state[0, rows, cc] = mean
                state[1, rows, cc] = one
                state[2, rows, cc] = two
            else:
                last[0, rows, cc] = track
                last[1, rows, cc] = mix
        if k + 1 < steps:
            start_gossip(k + 1, c)
        if k + 2 == steps:
            result(c, 2).start()
            result(c, 3).start()
        if k + 1 == steps:
            result(c, 0).start()
            result(c, 1).start()

    def result(c, n):
        src = last.at[n, :, cols(c)] if n < 2 else state.at[n - 1, :, cols(c)]
        dst = (out_track, out_mix, out_one, out_two)[n].at[:, cols(c)]
        return pltpu.make_async_copy(src, dst, out_sem.at[c, n])

    every = range(len(chunks))
    grad_load(0).start()
    for c in every:
        state_load(c, 0).start()
        state_load(c, 1).start()
    for i in range(1, len(ITEMS)):
        grad_load(i).start()
    for c in every:
        for n in range(2, 5):
            state_load(c, n).start()

    phases = (None, phase_one, phase_two, phase_three, phase_four)
    fill(0)
    pl.semaphore_wait(barrier, len(feeders))
    for phase, i in PROGRAM:
        if phase == 0:
            state_load(i, 0).wait()
            state_load(i, 1).wait()
            start_gossip(0, i)
        elif phase == 5:
            relay(i)
        else:
            phases[phase](i)
            if phase == 1 and i + 1 < len(ITEMS):
                fill(i + 1)

    for c in every:
        for n in range(4):
            result(c, n).wait()
    for cp in sent:
        cp.wait_send()
    for k in range(steps):
        for c in every:
            gossip(k, c).wait_send()
            if hops[k] != shifts[k]:
                gossip(k, c, False).wait_send()


def finish(track, mix, first, second, params, change, one, two):
    one[...] = BETA_ONE * first[...] + (1.0 - BETA_ONE) * track[...]
    two[...] = BETA_TWO * second[...] + (1.0 - BETA_TWO) * track[...] * track[...]
    weights = mix[...] - LEARNING_RATE * one[...] / (jnp.sqrt(two[...]) + EPSILON)
    change[...] = (weights - params[...]) / LEARNING_RATE


def per_device(params, tracker, last_grad, first_moment, second_moment, local_grads):
    rows, width = params.shape[1:]
    steps = local_grads.shape[0]
    shards = lax.axis_size("fsdp")
    replicas = lax.axis_size("replica")
    chunks = [(sum(WIDTHS[:c]), w) for c, w in enumerate(WIDTHS)]
    assert sum(WIDTHS) == width and len(ITEMS) == steps * len(WIDTHS)
    count = len(ITEMS)
    f32 = jnp.float32
    any_spec = pl.BlockSpec(memory_space=pl.ANY)
    track, mix, one, two = pl.pallas_call(
        functools.partial(kernel, steps, replicas, shards, chunks),
        out_shape=(jax.ShapeDtypeStruct((rows, width), f32),) * 4,
        in_specs=[any_spec] * 6,
        out_specs=(any_spec,) * 4,
        scratch_shapes=[
            pltpu.VMEM((steps, shards, rows, width), jnp.bfloat16),
            pltpu.VMEM((3, rows, width), f32),
            pltpu.VMEM((steps, 2, rows, width), f32),
            pltpu.VMEM((steps, 2, rows, width), f32),
            pltpu.VMEM((2, rows, width), f32),
            pltpu.VMEM((steps, 16, width), f32),
            pltpu.VMEM((steps, 2, 32, width), f32),
            pltpu.VMEM((steps, 16, width), f32),
            pltpu.VMEM((steps, 16, width), f32),
            pltpu.VMEM((steps, 2, 32, width), f32),
            pltpu.VMEM((steps, 2, 8, width), f32),
            pltpu.VMEM((steps, 16, width), f32),
            pltpu.VMEM((steps, 2, 16, width), f32),
            pltpu.SemaphoreType.DMA((count,)),
            pltpu.SemaphoreType.DMA((len(chunks), 5)),
            pltpu.SemaphoreType.DMA((len(chunks), 4)),
            pltpu.SemaphoreType.DMA((count, 8)),
            pltpu.SemaphoreType.DMA((count, 8)),
            pltpu.SemaphoreType.DMA((steps, len(chunks))),
            pltpu.SemaphoreType.DMA((steps, len(chunks))),
            pltpu.VMEM((1, 2, rows, width), f32),
            pltpu.SemaphoreType.DMA((steps, len(chunks))),
            pltpu.SemaphoreType.DMA((steps, len(chunks))),
        ],
        compiler_params=pltpu.CompilerParams(
            collective_id=0, has_side_effects=True, vmem_limit_bytes=60 << 20
        ),
        name="gossip_window",
    )(
        params[0], tracker[0], last_grad[0], first_moment[0], second_moment[0],
        local_grads.reshape(steps, shards, rows, width),
    )
    tile = pl.BlockSpec((rows, width // FINISH_TILES), lambda c: (0, c))
    block = jax.ShapeDtypeStruct((rows, width), f32)
    change, one, two = pl.pallas_call(
        finish,
        grid=(FINISH_TILES,),
        out_shape=(block,) * 3,
        in_specs=[tile] * 5,
        out_specs=(tile,) * 3,
        name="finish",
    )(track, mix, one, two, params[0])
    return change[None], one[None], two[None]


def solution(mesh):
    in_specs = (P("replica", "fsdp", None),) * 5 + (P(None, "replica", "fsdp", None, None),)
    out_specs = (P("replica", "fsdp", None),) * 3
    return jax.shard_map(
        per_device, mesh=mesh, in_specs=in_specs, out_specs=out_specs, check_vma=False
    )
```

```python
import functools

import jax
import jax.numpy as jnp
from jax import lax
from jax.experimental import pallas as pl
from jax.experimental.pallas import tpu as pltpu
from jax.sharding import PartitionSpec as P

LEARNING_RATE = 0.001
BETA_ONE = 0.9
BETA_TWO = 0.999
EPSILON = 1e-08

MESH = pl.DeviceIdType.MESH
RELAYED = (8,)
NX = 4
WIDTHS = [1152, 1152, 1024, 1024, 768]
ITEMS = [
    (0, 1), (0, 3), (1, 1), (1, 3), (2, 1), (0, 2), (2, 3), (0, 0), (1, 2), (0, 4), (1, 0), (2, 2), (1, 4),
    (2, 0), (2, 4), (3, 2), (3, 1), (3, 0), (3, 3), (3, 4),
]
X_FIRST = [5, 3, 11, 6]
PROGRAM = [
    (1, 0), (0, 0), (1, 1), (1, 2), (2, 0), (1, 3), (0, 1), (0, 3), (2, 1), (3, 0), (1, 4), (2, 2), (3, 1),
    (4, 0), (0, 4), (1, 5), (2, 3), (3, 2), (4, 1), (2, 4), (1, 6), (2, 5), (3, 3), (0, 2), (4, 2), (3, 4),
    (2, 6), (1, 7), (1, 8), (4, 3), (3, 5), (4, 4), (1, 9), (3, 6), (2, 7), (1, 10), (4, 5), (2, 8), (4, 6),
    (3, 7), (2, 9), (1, 11), (5, 1), (3, 8), (2, 10), (4, 7), (1, 12), (2, 11), (5, 3), (3, 9), (3, 10), (1,
    13), (1, 14), (4, 8), (3, 11), (4, 9), (2, 12), (4, 10), (2, 13), (1, 15), (3, 12), (4, 11), (2, 14), (3,
    13), (1, 16), (4, 12), (1, 17), (3, 14), (2, 15), (4, 13), (1, 18), (5, 2), (1, 19), (4, 14), (2, 16), (2,
    17), (5, 0), (2, 18), (2, 19), (3, 15), (3, 16), (3, 17), (5, 4), (3, 18), (3, 19), (4, 15), (4, 16), (4,
    17), (4, 18), (4, 19),
]
FINISH_TILES = 2


def kernel(
    steps, replicas, shards, chunks,
    params, tracker, last_grad, first_moment, second_moment, grads,
    out_track, out_mix, out_one, out_two,
    gbuf, state, tw, twr, last, s1, sx, q, ra, rx, rd, re, rc,
    load_sem, state_sem, out_sem, send_sem, recv_sem, gsend_sem, grecv_sem, hop, hsend_sem, hrecv_sem,
):
    f32 = jnp.float32
    r = lax.axis_index("replica")
    f = lax.axis_index("fsdp")
    y = f // NX
    x = lax.rem(f, NX)
    xm = lax.rem(x + NX - 1, NX)
    xp = lax.rem(x + 1, NX)
    x2 = lax.rem(x + 2, NX)
    oy = 1 - y

    def block(bx, by):
        return by * NX + bx

    to_xm = (r, block(xm, y))
    to_xp = (r, block(xp, y))
    to_y = (r, block(x, oy))
    sides = ((xm, to_xm), (xp, to_xp))
    low, high = slice(0, 8), slice(8, 16)
    shifts = [2 ** (k % (replicas.bit_length() - 1)) for k in range(steps)]
    hops = [shifts[k] // 2 if shifts[k] in RELAYED else shifts[k] for k in range(steps)]

    barrier = pltpu.get_barrier_semaphore()
    feeders = [to_xm, to_xp, to_y]
    feeders += [(lax.rem(r + replicas - s, replicas), f) for s in sorted(set(hops))]
    for dev in feeders:
        pl.semaphore_signal(barrier, inc=1, device_id=dev, device_id_type=MESH)

    def cols(c):
        return pl.ds(chunks[c][0], chunks[c][1])

    def state_load(c, n):
        src = (tracker, params, last_grad, first_moment, second_moment)[n]
        dst = tw.at[0, n, :, cols(c)] if n < 2 else state.at[n - 2, :, cols(c)]
        return pltpu.make_async_copy(src.at[:, cols(c)], dst, state_sem.at[c, n])

    def grad_load(i):
        k, c = ITEMS[i]
        return pltpu.make_async_copy(grads.at[k, :, :, cols(c)], gbuf.at[k, :, :, cols(c)], load_sem.at[i])

    sent = []

    def send(i, n, src, dst, dev):
        cp = pltpu.make_async_remote_copy(
            src_ref=src, dst_ref=dst, send_sem=send_sem.at[i, n], recv_sem=recv_sem.at[i, n],
            device_id=dev, device_id_type=MESH,
        )
        cp.start()
        sent.append(cp)

    def arrived(i, n, dst):
        pltpu.make_async_copy(dst, dst, recv_sem.at[i, n]).wait()

    def gossip(k, c, final=True):
        direct = final and hops[k] == shifts[k]
        src = tw if direct or not final else hop
        dst = twr if final else hop
        sems = (gsend_sem, grecv_sem) if final else (hsend_sem, hrecv_sem)
        return pltpu.make_async_remote_copy(
            src_ref=(src.at[k] if src is tw else src.at[0]).at[:, :, cols(c)],
            dst_ref=(dst.at[k] if dst is twr else dst.at[0]).at[:, :, cols(c)],
            send_sem=sems[0].at[k, c], recv_sem=sems[1].at[k, c],
            device_id=(lax.rem(r + hops[k], replicas), f), device_id_type=MESH,
        )

    def start_gossip(k, c):
        gossip(k, c, hops[k] == shifts[k]).start()

    def relay(c):
        for k in range(steps):
            if hops[k] != shifts[k]:
                gossip(k, c, False).wait_recv()
                gossip(k, c).start()

    def raw(i, bx, by):
        k, c = ITEMS[i]
        return gbuf[k, block(bx, by), :, cols(c)].astype(f32)

    def fill(i):
        k, c = ITEMS[i]
        cc = cols(c)
        grad_load(i).wait()
        if i in X_FIRST:
            for n, (bx, _) in enumerate(sides):
                ours, theirs = (low, high) if n == 0 else (high, low)
                for b, by in enumerate((y, oy)):
                    sx[k, n, 8 * b : 8 * b + 8, cc] = raw(i, x2, by)[ours]
                    sx[k, n, 16 + 8 * b : 24 + 8 * b, cc] = raw(i, bx, by)[theirs]
        else:
            s1[k, :, cc] = raw(i, x2, oy)
            for n, (bx, _) in enumerate(sides):
                sx[k, n, 0:16, cc] = raw(i, bx, oy)
                sx[k, n, 16:24, cc] = raw(i, bx, y)[high if n == 0 else low]

    def phase_one(i):
        k, c = ITEMS[i]
        cc = cols(c)
        if i in X_FIRST:
            for n, (_, dev) in enumerate(sides):
                send(i, 3 + n, sx.at[k, n, 0:16, cc], rx.at[k, n, 0:16, cc], dev)
            for n, (_, dev) in enumerate(sides):
                send(i, 1 + n, sx.at[k, n, 16:32, cc], rx.at[k, n, 16:32, cc], dev)
        else:
            send(i, 0, s1.at[k, :, cc], ra.at[k, :, cc], to_y)
            for n, (_, dev) in enumerate(sides):
                send(i, 1 + n, sx.at[k, n, 0:24, cc], rx.at[k, n, 0:24, cc], dev)

    def phase_two(i):
        k, c = ITEMS[i]
        cc = cols(c)
        if i in X_FIRST:
            for n, (bx, dev) in enumerate(sides):
                arrived(i, 3 + n, rx.at[k, n, 0:16, cc])
                for b, by in enumerate((y, oy)):
                    rows = slice(8 * b, 8 * b + 8)
                    rx[k, n, rows, cc] = rx[k, n, rows, cc] + raw(i, bx, by)[low if n == 0 else high]
                send(i, 6 + n, rx.at[k, n, 0:16, cc], rc.at[k, n, :, cc], dev)
        else:
            arrived(i, 0, ra.at[k, :, cc])
            ra[k, :, cc] = ra[k, :, cc] + raw(i, x2, y)
            for n, (_, dev) in enumerate(sides):
                send(i, 3 + n, ra.at[k, 8 * n : 8 * n + 8, cc], rd.at[k, n, :, cc], dev)
            for n in range(2):
                arrived(i, 1 + n, rx.at[k, n, 0:24, cc])
            q[k, :, cc] = raw(i, x, oy) + rx[k, 0, 0:16, cc] + rx[k, 1, 0:16, cc]
            send(i, 5, q.at[k, :, cc], re.at[k, :, cc], to_y)

    def phase_three(i):
        k, c = ITEMS[i]
        cc = cols(c)
        if i in X_FIRST:
            for n in range(2):
                arrived(i, 1 + n, rx.at[k, n, 16:32, cc])
                arrived(i, 6 + n, rc.at[k, n, :, cc])
            mine = raw(i, x, oy)
            q[k, 0:8, cc] = mine[low] + rc[k, 0, 8:16, cc] + rx[k, 1, 24:32, cc]
            q[k, 8:16, cc] = mine[high] + rx[k, 0, 24:32, cc] + rc[k, 1, 8:16, cc]
            send(i, 5, q.at[k, :, cc], re.at[k, :, cc], to_y)
        else:
            for n, (bx, dev) in enumerate(sides):
                arrived(i, 3 + n, rd.at[k, n, :, cc])
                rd[k, n, :, cc] = rd[k, n, :, cc] + raw(i, bx, y)[low if n == 0 else high]
                send(i, 6 + n, rd.at[k, n, :, cc], rc.at[k, n, 0:8, cc], dev)

    def phase_four(i):
        k, c = ITEMS[i]
        cc = cols(c)
        if i not in X_FIRST:
            for n in range(2):
                arrived(i, 6 + n, rc.at[k, n, 0:8, cc])
        if k == 0:
            for n in range(2, 5):
                state_load(c, n).wait()
        gossip(k, c).wait_recv()
        arrived(i, 5, re.at[k, :, cc])
        mine = raw(i, x, y)
        for h, rows in enumerate((low, high)):
            near = rx[k, 1 - h, 16:24, cc]
            mean = (mine[rows] + rc[k, h, 0:8, cc] + near + re[k, rows, cc]) * (1.0 / shards)
            track = 0.5 * (tw[k, 0, rows, cc] + twr[k, 0, rows, cc]) + mean - state[0, rows, cc]
            mix = 0.5 * (tw[k, 1, rows, cc] + twr[k, 1, rows, cc])
            if k + 1 < steps:
                one = BETA_ONE * state[1, rows, cc] + (1.0 - BETA_ONE) * track
                two = BETA_TWO * state[2, rows, cc] + (1.0 - BETA_TWO) * track * track
                tw[k + 1, 0, rows, cc] = track
                tw[k + 1, 1, rows, cc] = mix - LEARNING_RATE * one / (jnp.sqrt(two) + EPSILON)
                state[0, rows, cc] = mean
                state[1, rows, cc] = one
                state[2, rows, cc] = two
            else:
                last[0, rows, cc] = track
                last[1, rows, cc] = mix
        if k + 1 < steps:
            start_gossip(k + 1, c)
        if k + 2 == steps:
            result(c, 2).start()
            result(c, 3).start()
        if k + 1 == steps:
            result(c, 0).start()
            result(c, 1).start()

    def result(c, n):
        src = last.at[n, :, cols(c)] if n < 2 else state.at[n - 1, :, cols(c)]
        dst = (out_track, out_mix, out_one, out_two)[n].at[:, cols(c)]
        return pltpu.make_async_copy(src, dst, out_sem.at[c, n])

    every = range(len(chunks))
    grad_load(0).start()
    for c in every:
        state_load(c, 0).start()
        state_load(c, 1).start()
    for i in range(1, len(ITEMS)):
        grad_load(i).start()
    for c in every:
        for n in range(2, 5):
            state_load(c, n).start()

    phases = (None, phase_one, phase_two, phase_three, phase_four)
    fill(0)
    pl.semaphore_wait(barrier, len(feeders))
    for phase, i in PROGRAM:
        if phase == 0:
            state_load(i, 0).wait()
            state_load(i, 1).wait()
            start_gossip(0, i)
        elif phase == 5:
            relay(i)
        else:
            phases[phase](i)
            if phase == 1 and i + 1 < len(ITEMS):
                fill(i + 1)

    for c in every:
        for n in range(4):
            result(c, n).wait()
    for cp in sent:
        cp.wait_send()
    for k in range(steps):
        for c in every:
            gossip(k, c).wait_send()
            if hops[k] != shifts[k]:
                gossip(k, c, False).wait_send()


def finish(track, mix, first, second, params, change, one, two):
    one[...] = BETA_ONE * first[...] + (1.0 - BETA_ONE) * track[...]
    two[...] = BETA_TWO * second[...] + (1.0 - BETA_TWO) * track[...] * track[...]
    weights = mix[...] - LEARNING_RATE * one[...] / (jnp.sqrt(two[...]) + EPSILON)
    change[...] = (weights - params[...]) / LEARNING_RATE


def per_device(params, tracker, last_grad, first_moment, second_moment, local_grads):
    rows, width = params.shape[1:]
    steps = local_grads.shape[0]
    shards = lax.axis_size("fsdp")
    replicas = lax.axis_size("replica")
    chunks = [(sum(WIDTHS[:c]), w) for c, w in enumerate(WIDTHS)]
    assert sum(WIDTHS) == width and len(ITEMS) == steps * len(WIDTHS)
    count = len(ITEMS)
    f32 = jnp.float32
    any_spec = pl.BlockSpec(memory_space=pl.ANY)
    track, mix, one, two = pl.pallas_call(
        functools.partial(kernel, steps, replicas, shards, chunks),
        out_shape=(jax.ShapeDtypeStruct((rows, width), f32),) * 4,
        in_specs=[any_spec] * 6,
        out_specs=(any_spec,) * 4,
        scratch_shapes=[
            pltpu.VMEM((steps, shards, rows, width), jnp.bfloat16),
            pltpu.VMEM((3, rows, width), f32),
            pltpu.VMEM((steps, 2, rows, width), f32),
            pltpu.VMEM((steps, 2, rows, width), f32),
            pltpu.VMEM((2, rows, width), f32),
            pltpu.VMEM((steps, 16, width), f32),
            pltpu.VMEM((steps, 2, 32, width), f32),
            pltpu.VMEM((steps, 16, width), f32),
            pltpu.VMEM((steps, 16, width), f32),
            pltpu.VMEM((steps, 2, 32, width), f32),
            pltpu.VMEM((steps, 2, 8, width), f32),
            pltpu.VMEM((steps, 16, width), f32),
            pltpu.VMEM((steps, 2, 16, width), f32),
            pltpu.SemaphoreType.DMA((count,)),
            pltpu.SemaphoreType.DMA((len(chunks), 5)),
            pltpu.SemaphoreType.DMA((len(chunks), 4)),
            pltpu.SemaphoreType.DMA((count, 8)),
            pltpu.SemaphoreType.DMA((count, 8)),
            pltpu.SemaphoreType.DMA((steps, len(chunks))),
            pltpu.SemaphoreType.DMA((steps, len(chunks))),
            pltpu.VMEM((1, 2, rows, width), f32),
            pltpu.SemaphoreType.DMA((steps, len(chunks))),
            pltpu.SemaphoreType.DMA((steps, len(chunks))),
        ],
        compiler_params=pltpu.CompilerParams(
            collective_id=0, has_side_effects=True, vmem_limit_bytes=60 << 20
        ),
        name="gossip_window",
    )(
        params[0], tracker[0], last_grad[0], first_moment[0], second_moment[0],
        local_grads.reshape(steps, shards, rows, width),
    )
    tile = pl.BlockSpec((rows, width // FINISH_TILES), lambda c: (0, c))
    block = jax.ShapeDtypeStruct((rows, width), f32)
    change, one, two = pl.pallas_call(
        finish,
        grid=(FINISH_TILES,),
        out_shape=(block,) * 3,
        in_specs=[tile] * 5,
        out_specs=(tile,) * 3,
        name="finish",
    )(track, mix, one, two, params[0])
    return change[None], one[None], two[None]


def solution(mesh):
    in_specs = (P("replica", "fsdp", None),) * 5 + (P(None, "replica", "fsdp", None, None),)
    out_specs = (P("replica", "fsdp", None),) * 3
    return jax.shard_map(
        per_device, mesh=mesh, in_specs=in_specs, out_specs=out_specs, check_vma=False
    )
```
